32 devices in a mesh: rep: 2 (over x), frame: 16 (over z, y, core).
Axes of the slice: x: 2, y: 2, z: 4, core: 2. Of those that a mesh axis runs over, the one named last changes fastest.
Arguments:
- queries: bfloat16 [12288, 1536], P(('rep', 'frame')), parts along dimension 0, may hold values from -9 to 9
- keys: bfloat16 [12288, 1536], P(('rep', 'frame')), parts along dimension 0, may hold values from -6 to 6
- values: bfloat16 [12288, 1536], P(('rep', 'frame')), parts along dimension 0, may hold values from -6 to 6
- out_grad: bfloat16 [12288, 1536], P(('rep', 'frame')), parts along dimension 0, may hold values from -6 to 6
- key_blocks: int32 [32, 18], P('rep'), parts along dimension 0, may hold values from -1 to 95, as said below
- seed_offsets: int32 [192], P(('rep', 'frame')), parts along dimension 0, may hold values from 0 to 1048575
- dropout_seed: int32 [2], P('rep'), parts along dimension 0, may hold values from 0 to 1073741823
Outputs:
- attended: bfloat16 [12288, 1536], P(('rep', 'frame')), parts along dimension 0
- query_grad: bfloat16 [12288, 1536], P(('rep', 'frame')), parts along dimension 0
- key_grad: bfloat16 [12288, 1536], P(('rep', 'frame')), parts along dimension 0
- value_grad: bfloat16 [12288, 1536], P(('rep', 'frame')), parts along dimension 0
The draws below stay inside these ranges and needn't reach their ends.
There are 2 independent parts, one for each index of `rep`. The reference program is written for one: setup_inputs(seed, part) draws one part's arguments, and reference() takes and returns one part's arrays. A program takes and returns all parts, laid end to end along the dimension named above; each array names one. Nothing has to cross between parts.
Inputs may be any that keep to these rules, and one draw needn't show every extreme that they name: `key_blocks`: row r lists the key blocks read by the queries of tokens r * 384 to r * 384 + 383: first the 6 blocks of range r in order; then for each level l from 0 to 3 a window of range r - 2 ** l and then one of range r + 2 ** l, each of max(6 // 2 ** (l + 1), 1) blocks of that range consecutive modulo 6, or -1 in every entry of a window whose range lies outside the video.
All inputs are finite; a program needn't handle non-finite values.
Results may differ from the reference program's by a relative error of at most 0.0056.
Values may be sent and summed in bfloat16 or wider, within the bound.
A program may use at most 128 MiB of HBM per device.

```python
import math
import jax
import jax.numpy as jnp
from jax import lax

H = 12
HD = 128
BLOCK = 64
LEVELS = 4
BLK_DEV = 6
TOK_DEV = 384
TOKENS = 6144
NQB = 96
NKEY = 18
N_FRAME = 16


def draw_queries(key, part):
    base_draw = 1.5 * jnp.clip(jax.random.normal(jax.random.fold_in(key, 5), (TOKENS, H * HD), jnp.float32), -6.0, 6.0)
    return base_draw.astype(jnp.bfloat16)


def draw_keys(key, part):
    base_draw = jnp.clip(jax.random.normal(jax.random.fold_in(key, 8), (TOKENS, H * HD), jnp.float32), -6.0, 6.0)
    return base_draw.astype(jnp.bfloat16)


def draw_key_blocks(key, part):
    frame_ranks = jnp.arange(N_FRAME, dtype=jnp.int32)
    pieces = [frame_ranks[:, None] * BLK_DEV + jnp.arange(BLK_DEV, dtype=jnp.int32)[None, :]]
    for depth_level in range(LEVELS):
        block_count = max(BLK_DEV >> depth_level + 1, 1)
        for side_sign in (-1, 1):
            peer_ranks = frame_ranks + side_sign * 2 ** depth_level
            starts = jax.random.randint(jax.random.fold_in(key, 10 * depth_level + side_sign + 5), (N_FRAME, 1), 0, BLK_DEV)
            block_ids = peer_ranks[:, None] * BLK_DEV + (starts + jnp.arange(block_count, dtype=jnp.int32)[None, :]) % BLK_DEV
            inside = (peer_ranks >= 0) & (peer_ranks < N_FRAME)
            pieces.append(jnp.where(inside[:, None], block_ids, -1))
    return jnp.concatenate(pieces, axis=1).astype(jnp.int32)


def set_ends(entries, key, low, high):
    longest = entries.shape.index(max(entries.shape))
    spots = []
    for shift in (0, 1):
        where = [jax.random.randint(jax.random.fold_in(key, axis), (), 0, length) for axis, length in enumerate(entries.shape)]
        where[longest] = (where[longest] + shift) % entries.shape[longest]
        spots.append(tuple(where))
    return entries.at[spots[0]].set(low).at[spots[1]].set(high)


def steps_of(rng, extent, cuts, smallest, high):
    def one(dim, parts):
        heights = jax.random.uniform(jax.random.fold_in(jax.random.fold_in(rng, 6), dim), (parts,), jnp.float32, smallest / len(cuts), high / len(cuts))
        return jnp.repeat(jnp.exp(heights), extent[dim] // parts).reshape((-1,) + (1,) * (len(extent) - dim - 1))

    gain = one(*cuts[0])
    for cut in cuts[1:]:
        gain = gain * one(*cut)
    return gain


def bell_draw(stream_key, extent, width, limit, split=(), held_as=jnp.bfloat16):
    values = jax.random.normal(stream_key, extent, jnp.float32) * width
    if len(split) > 0:
        values = steps_of(stream_key, extent, split, -0.22, 0.18) * values
    return jnp.clip(values, min=-limit, max=limit).astype(held_as)


def setup_inputs(seed: int = 0, part: int = 0) -> dict:
    streams_of = jax.random.split(jax.random.key(seed), 8)
    own_keys = jax.random.split(jax.random.fold_in(streams_of[7], part), 8)
    queries = draw_queries(jax.random.fold_in(jax.random.fold_in(streams_of[7], part), 71), part)
    keys = draw_keys(jax.random.fold_in(jax.random.fold_in(streams_of[7], part), 71), part)
    values = bell_draw(own_keys[2], (TOKENS, H * HD), 1.0, 6.0, ((0, 16),))
    out_grad = bell_draw(own_keys[3], (TOKENS, H * HD), 1.0, 6.0, ((0, 16),))
    key_blocks = draw_key_blocks(jax.random.fold_in(jax.random.fold_in(streams_of[7], part), 71), part)
    seed_offsets = set_ends(jax.random.randint(own_keys[5], (NQB,), 0, 1048576), jax.random.fold_in(own_keys[5], 1), 0, 1048575).astype(jnp.int32)
    dropout_seed = jax.random.randint(own_keys[6], (1,), 0, 1073741824).astype(jnp.int32)
    return dict(queries=queries, keys=keys, values=values, out_grad=out_grad, key_blocks=key_blocks, seed_offsets=seed_offsets, dropout_seed=dropout_seed)


KEEP_SCALE = 1.0 / 0.9

def logical_right(number, amount):
    return lax.shift_right_logical(number, jnp.full_like(number, amount))

def mixing(number):
    number = number * -1640531535
    number = number ^ logical_right(number, 16)
    number = number * 739982445
    number = number ^ logical_right(number, 15)
    return number

def round_trip(number):
    return lax.optimization_barrier(number.astype(jnp.bfloat16)).astype(jnp.float32)

def reference(queries, keys, values, out_grad, key_blocks, seed_offsets, dropout_seed):
    row_width = H * HD
    score_scale = 1.0 / math.sqrt(HD)
    within = jnp.arange(BLOCK, dtype=jnp.int32)
    head_ids = jnp.arange(H, dtype=jnp.int32)
    remote_rows = jnp.arange(NKEY * BLOCK, dtype=jnp.int32) >= TOK_DEV

    def one_range(loop_state, range_id):
        key_total, value_total = loop_state
        listed = key_blocks[range_id]
        alive_slots = listed >= 0
        safe_ids = jnp.where(alive_slots, listed, 0)
        key_tokens = (safe_ids[:, None] * BLOCK + within[None, :]).reshape(-1)
        alive_tokens = jnp.repeat(alive_slots, BLOCK)
        first_row = (range_id * TOK_DEV).astype(jnp.int32)
        query_tokens = first_row + jnp.arange(TOK_DEV, dtype=jnp.int32)
        query_rows = lax.dynamic_slice_in_dim(queries, first_row, TOK_DEV, 0).astype(jnp.float32).reshape(TOK_DEV, H, HD)
        grad_rows = lax.dynamic_slice_in_dim(out_grad, first_row, TOK_DEV, 0).astype(jnp.float32).reshape(TOK_DEV, H, HD)
        key_rows = keys[key_tokens].astype(jnp.float32).reshape(-1, H, HD)
        value_rows = values[key_tokens].astype(jnp.float32).reshape(-1, H, HD)
        scores = jnp.einsum('qhd,khd->hqk', query_rows, key_rows) * score_scale
        scores = jnp.where(alive_tokens[None, None, :], scores, -jnp.inf)
        row_top = lax.optimization_barrier(jnp.max(scores, axis=2, keepdims=True))
        log_total = row_top + jnp.log(lax.optimization_barrier(jnp.sum(jnp.exp(scores - row_top), axis=2, keepdims=True)))
        weights = jnp.exp(scores - log_total)
        row_keys = mixing(dropout_seed[0] + seed_offsets[query_tokens // BLOCK] + query_tokens * 7919)
        hashed = mixing(row_keys[None, :, None] ^ key_tokens[None, None, :] * 40503 + head_ids[:, None, None] * 977)
        dropped = jnp.where(logical_right(hashed, 16) & 1023 >= 102, KEEP_SCALE, 0.0).astype(jnp.float32)
        drop_probs = round_trip(weights * dropped)
        attended = jnp.einsum('hqk,khd->qhd', drop_probs, value_rows).reshape(TOK_DEV, row_width).astype(jnp.bfloat16)
        grad_probs = jnp.einsum('qhd,khd->hqk', grad_rows, value_rows) * dropped
        row_delta = lax.optimization_barrier(jnp.sum(weights * grad_probs, axis=2, keepdims=True))
        score_grad = round_trip(weights * (grad_probs - row_delta) * score_scale)
        query_grad = jnp.einsum('hqk,khd->qhd', score_grad, key_rows).reshape(TOK_DEV, row_width).astype(jnp.bfloat16)
        key_part = jnp.einsum('hqk,qhd->khd', score_grad, query_rows).reshape(-1, row_width)
        value_part = jnp.einsum('hqk,qhd->khd', drop_probs, grad_rows).reshape(-1, row_width)
        key_part = jnp.where(remote_rows[:, None], round_trip(key_part), key_part)
        value_part = jnp.where(remote_rows[:, None], round_trip(value_part), value_part)
        key_total = key_total.at[key_tokens].add(key_part)
        value_total = value_total.at[key_tokens].add(value_part)
        return ((key_total, value_total), (attended, query_grad))
    zero_rows = jnp.zeros((TOKENS, row_width), jnp.float32)
    (key_total, value_total), (attended, query_grad) = lax.scan(one_range, (zero_rows, zero_rows), jnp.arange(N_FRAME, dtype=jnp.int32))
    return (attended.reshape(TOKENS, row_width), query_grad.reshape(TOKENS, row_width), key_total.astype(jnp.bfloat16), value_total.astype(jnp.bfloat16))
```

```python
import functools
import math

import jax
import jax.numpy as jnp
from jax import lax
from jax.experimental import pallas as pl
from jax.experimental.pallas import tpu as pltpu
from jax.sharding import PartitionSpec as P

HD = 128
BLOCK = 64
LEVELS = 4
KEEP_SCALE = 1.0 / 0.9
CHUNKS = 3
ROWS = 128


def logical_right(number, amount):
    return lax.shift_right_logical(number, jnp.full_like(number, amount))


def mixing(number):
    number = number * -1640531535
    number = number ^ logical_right(number, 16)
    number = number * 739982445
    number = number ^ logical_right(number, 15)
    return number


def plan_windows(blocks_dev):
    entries = []
    slot_start = blocks_dev
    for depth_level in range(LEVELS):
        block_count = max(blocks_dev >> depth_level + 1, 1)
        distance = 2**depth_level
        entries.append((distance, slot_start, block_count))
        entries.append((-distance, slot_start + block_count, block_count))
        slot_start = slot_start + 2 * block_count
    return entries


def shift(value, by):
    size = lax.axis_size("frame")
    pairs = [(i, i + by) for i in range(size) if 0 <= i + by < size]
    return lax.ppermute(value, "frame", pairs)


def sender_ids(key_blocks, frame_rank, frames, blocks_dev, shift_by, slot_start, block_count):
    reader = jnp.clip(frame_rank + shift_by, 0, frames - 1)
    reader_row = lax.dynamic_slice_in_dim(key_blocks, reader, 1, 0)[0]
    listed = reader_row[slot_start : slot_start + block_count]
    return jnp.clip(listed - frame_rank * blocks_dev, 0, blocks_dev - 1)


def pack_kernel(counts, ids_ref, k_ref, v_ref, *out_refs):
    at = 0
    for out_ref, count in zip(out_refs, counts):
        for j in range(count):
            start = pl.multiple_of(ids_ref[at] * BLOCK, BLOCK)
            at += 1
            rows = slice(j * BLOCK, (j + 1) * BLOCK)
            out_ref[0, rows, :] = k_ref[pl.ds(start, BLOCK), :]
            out_ref[1, rows, :] = v_ref[pl.ds(start, BLOCK), :]


def contract(a, b, dim_a, dim_b):
    return lax.dot_general(
        a, b, (((dim_a,), (dim_b,)), ((), ())), preferred_element_type=jnp.float32
    )


def fold_rows(x, op):
    total = x[0:8]
    for r in range(8, x.shape[0], 8):
        total = op(total, x[r : r + 8])
    return total


def main_kernel(spans, first_head, n_alias, *refs):
    n_win = len(spans)
    rk_ref, kt_ref, bias_ref, q_ref, k_ref, v_ref, do_ref = refs[:7]
    win_refs = refs[7 : 7 + n_win]
    outs = refs[7 + n_win + n_alias :]
    att_ref, dq_ref, own_ref = outs[:3]
    back_refs = outs[3 : 3 + n_win]
    kall, vall, s_ref, dp_ref, pd_ref, ds_ref, gk_ref, gv_ref = outs[3 + n_win :]
    tok = q_ref.shape[0]
    slots = kall.shape[0]
    score_scale = 1.0 / math.sqrt(HD)
    exp_scale = score_scale * math.log2(math.e)
    steps = slots // ROWS
    tiles = tok // 128

    kall[0:tok, :] = k_ref[...]
    vall[0:tok, :] = v_ref[...]
    for win_ref, (lo, hi) in zip(win_refs, spans):
        kall[lo:hi, :] = win_ref[0]
        vall[lo:hi, :] = win_ref[1]

    def rows_of(j):
        return pl.ds(pl.multiple_of(j * ROWS, ROWS), ROWS)

    def pass_a(j, top):
        rows = rows_of(j)
        raw = contract(kall[rows, :], q_ref[...], 1, 1)
        bias = bias_ref[rows, :]
        new_top = []
        for t in range(tiles):
            lanes = slice(t * 128, (t + 1) * 128)
            s = raw[:, lanes] + bias
            s_ref[rows, lanes] = s
            new_top.append(jnp.maximum(top[t], fold_rows(s, jnp.maximum)))
        return tuple(new_top)

    top = lax.fori_loop(
        0, steps, pass_a, tuple(jnp.full((8, 128), -jnp.inf, jnp.float32) for _ in range(tiles))
    )
    top = [jnp.max(t, axis=0, keepdims=True) for t in top]
    head_term = (first_head + pl.program_id(0)) * 977
    row_keys = [rk_ref[:, t * 128 : (t + 1) * 128] for t in range(tiles)]

    def pass_b(j, sums):
        rows = rows_of(j)
        grads = contract(vall[rows, :], do_ref[...], 1, 1)
        token_term = kt_ref[rows, :] + head_term
        new_sums = []
        for t in range(tiles):
            lanes = slice(t * 128, (t + 1) * 128)
            e = jnp.exp2((s_ref[rows, lanes] - top[t]) * exp_scale)
            x = token_term ^ row_keys[t]
            x = x * -1640531535
            x = x ^ logical_right(x, 16)
            x = x * 739982445
            x = x ^ logical_right(x, 15)
            keep = (x & (1023 << 16)) >= (102 << 16)
            dp = grads[:, lanes]
            dp_ref[rows, lanes] = dp
            s_ref[rows, lanes] = jnp.where(keep, e, -e)
            kept = jnp.where(keep, e * dp, 0.0)
            new_sums.append(sums[2 * t] + fold_rows(e, jnp.add))
            new_sums.append(sums[2 * t + 1] + fold_rows(kept, jnp.add))
        return tuple(new_sums)

    sums = lax.fori_loop(
        0, steps, pass_b, tuple(jnp.zeros((8, 128), jnp.float32) for _ in range(2 * tiles))
    )
    sums = [jnp.sum(x, axis=0, keepdims=True) for x in sums]
    inv = [KEEP_SCALE / sums[2 * t] for t in range(tiles)]
    delta = [sums[2 * t + 1] * inv[t] * (inv[t] / KEEP_SCALE) for t in range(tiles)]

    def pass_c(j, _):
        rows = rows_of(j)
        for t in range(tiles):
            lanes = slice(t * 128, (t + 1) * 128)
            es = s_ref[rows, lanes]
            pd = jnp.maximum(es, 0.0) * inv[t]
            ds = pd * dp_ref[rows, lanes] - jnp.abs(es) * delta[t]
            pd_ref[rows, lanes] = pd.astype(jnp.bfloat16)
            ds_ref[rows, lanes] = ds.astype(jnp.bfloat16)
        gk_ref[rows, :] = contract(ds_ref[rows, :], q_ref[...], 1, 0) * score_scale
        gv_ref[rows, :] = contract(pd_ref[rows, :], do_ref[...], 1, 0)
        return 0

    lax.fori_loop(0, steps, pass_c, 0)
    att_ref[...] = contract(pd_ref[...], vall[...], 0, 0).astype(jnp.bfloat16)
    dq_ref[...] = (contract(ds_ref[...], kall[...], 0, 0) * score_scale).astype(jnp.bfloat16)
    own_ref[0] = gk_ref[0:tok, :]
    own_ref[1] = gv_ref[0:tok, :]
    for back_ref, (lo, hi) in zip(back_refs, spans):
        back_ref[0] = gk_ref[lo:hi, :].astype(jnp.bfloat16)
        back_ref[1] = gv_ref[lo:hi, :].astype(jnp.bfloat16)


def finish_kernel(counts, n_alias, ids_ref, own_ref, *refs):
    ret_refs = refs[: len(counts)]
    kg_ref, vg_ref, acc = refs[len(counts) + n_alias :]
    acc[...] = own_ref[...]
    at = 0
    for ret_ref, count in zip(ret_refs, counts):
        for j in range(count):
            rows = pl.ds(pl.multiple_of(ids_ref[at] * BLOCK, BLOCK), BLOCK)
            at += 1
            acc[:, rows, :] += ret_ref[:, j * BLOCK : (j + 1) * BLOCK, :].astype(jnp.float32)
    kg_ref[...] = acc[0].astype(jnp.bfloat16)
    vg_ref[...] = acc[1].astype(jnp.bfloat16)


def local(queries, keys, values, out_grad, key_blocks, seed_offsets, dropout_seed):
    tok, width = queries.shape
    blocks_dev = tok // BLOCK
    heads = width // HD
    chunks = CHUNKS if heads % CHUNKS == 0 else 1
    nh = heads // chunks
    wc = nh * HD
    frames = lax.axis_size("frame")
    frame_rank = lax.axis_index("frame")
    entries = plan_windows(blocks_dev)
    counts = [count for _, _, count in entries]
    spans = [(start * BLOCK, (start + count) * BLOCK) for _, start, count in entries]
    slots = key_blocks.shape[1] * BLOCK
    ids = jnp.concatenate(
        [sender_ids(key_blocks, frame_rank, frames, blocks_dev, *entry) for entry in entries]
    )
    listed = lax.dynamic_slice_in_dim(key_blocks, frame_rank, 1, 0)[0]
    alive = listed >= 0
    tokens = (jnp.where(alive, listed, 0)[:, None] * BLOCK + jnp.arange(BLOCK, dtype=jnp.int32)).reshape(-1)
    token_terms = jnp.broadcast_to((tokens * 40503)[:, None], (slots, 128))
    bias = jnp.where(jnp.repeat(alive, BLOCK), 0.0, -jnp.inf).astype(jnp.float32)
    bias = jnp.broadcast_to(bias[:, None], (slots, 128))
    query_tokens = frame_rank * tok + jnp.arange(tok, dtype=jnp.int32)
    row_keys = mixing(dropout_seed[0] + jnp.repeat(seed_offsets, BLOCK) + query_tokens * 7919)[None, :]

    bf16, f32 = jnp.bfloat16, jnp.float32
    smem = pl.BlockSpec(memory_space=pltpu.SMEM)
    anyspec = pl.BlockSpec(memory_space=pl.ANY)
    win_shapes = [jax.ShapeDtypeStruct((2, n * BLOCK, wc), bf16) for n in counts]
    win_specs = [pl.BlockSpec((2, n * BLOCK, HD), lambda h: (0, 0, h)) for n in counts]
    full = jax.ShapeDtypeStruct((tok, width), bf16)

    arrived = []
    for c in range(chunks):
        column = pl.BlockSpec((tok, wc), lambda i, c=c: (0, c))
        packed = pl.pallas_call(
            functools.partial(pack_kernel, counts),
            grid=(1,),
            in_specs=[smem, column, column],
            out_specs=[pl.BlockSpec((2, n * BLOCK, wc), lambda i: (0, 0, 0)) for n in counts],
            out_shape=win_shapes,
            cost_estimate=pl.CostEstimate(flops=0, bytes_accessed=tok * wc * 12, transcendentals=0),
            name="pack",
        )(ids, keys, values)
        arrived.append([shift(p, e[0]) for p, e in zip(packed, entries)])

    outs = []
    owns = []
    returned = []
    for c in range(chunks):
        head = pl.BlockSpec((tok, HD), lambda h, c=c: (0, c * nh + h))
        n_alias = len(outs)
        n_in = 7 + len(entries)
        result = pl.pallas_call(
            functools.partial(main_kernel, spans, c * nh, n_alias),
            grid=(nh,),
            in_specs=[
                pl.BlockSpec((1, tok), lambda h: (0, 0)),
                pl.BlockSpec((slots, 128), lambda h: (0, 0)),
                pl.BlockSpec((slots, 128), lambda h: (0, 0)),
                head, head, head, head, *win_specs, *([anyspec] * n_alias),
            ],
            out_specs=[head, head, pl.BlockSpec((2, tok, HD), lambda h: (0, 0, h)), *win_specs],
            out_shape=[full, full, jax.ShapeDtypeStruct((2, tok, wc), f32), *win_shapes],
            scratch_shapes=[
                pltpu.VMEM((slots, HD), bf16),
                pltpu.VMEM((slots, HD), bf16),
                pltpu.VMEM((slots, tok), f32),
                pltpu.VMEM((slots, tok), f32),
                pltpu.VMEM((slots, tok), bf16),
                pltpu.VMEM((slots, tok), bf16),
                pltpu.VMEM((slots, HD), f32),
                pltpu.VMEM((slots, HD), f32),
            ],
            input_output_aliases={n_in + i: i for i in range(n_alias)},
            compiler_params=pltpu.CompilerParams(dimension_semantics=("arbitrary",)),
            cost_estimate=pl.CostEstimate(
                flops=nh * 12 * tok * slots * HD, bytes_accessed=nh * slots * HD * 16,
                transcendentals=nh * tok * slots,
            ),
            name="attend",
        )(row_keys, token_terms, bias, queries, keys, values, out_grad, *arrived[c], *outs)
        outs = list(result[:2])
        owns.append(result[2])
        returned.append([shift(p, -e[0]) for p, e in zip(result[3:], entries)])

    grads = []
    for c in range(chunks):
        head = pl.BlockSpec((tok, HD), lambda h, c=c: (0, c * nh + h))
        n_alias = len(grads)
        n_in = 2 + len(entries)
        grads = pl.pallas_call(
            functools.partial(finish_kernel, counts, n_alias),
            grid=(nh,),
            in_specs=[
                smem, pl.BlockSpec((2, tok, HD), lambda h: (0, 0, h)), *win_specs,
                *([anyspec] * n_alias),
            ],
            out_specs=[head, head],
            out_shape=[full, full],
            scratch_shapes=[pltpu.VMEM((2, tok, HD), f32)],
            input_output_aliases={n_in + i: i for i in range(n_alias)},
            compiler_params=pltpu.CompilerParams(dimension_semantics=("arbitrary",)),
            cost_estimate=pl.CostEstimate(
                flops=0, bytes_accessed=nh * slots * HD * 10, transcendentals=0
            ),
            name="finish",
        )(ids, owns[c], *returned[c], *grads)
    return (outs[0], outs[1], grads[0], grads[1])


def solution(mesh):
    rows = P(("rep", "frame"), None)
    return jax.shard_map(
        local,
        mesh=mesh,
        in_specs=(rows, rows, rows, rows, P("rep", None), P(("rep", "frame")), P("rep")),
        out_specs=(rows, rows, rows, rows),
        check_vma=False,
    )
```

```python
import functools
import math

import jax
import jax.numpy as jnp
from jax import lax
from jax.experimental import pallas as pl
from jax.experimental.pallas import tpu as pltpu
from jax.sharding import PartitionSpec as P

HD = 128
BLOCK = 64
LEVELS = 4
KEEP_SCALE = 1.0 / 0.9
ROWS = 128


def logical_right(number, amount):
    return lax.shift_right_logical(number, jnp.full_like(number, amount))


def mixing(number):
    number = number * -1640531535
    number = number ^ logical_right(number, 16)
    number = number * 739982445
    number = number ^ logical_right(number, 15)
    return number


def plan_windows(blocks_dev):
    entries = []
    slot_start = blocks_dev
    for depth_level in range(LEVELS):
        block_count = max(blocks_dev >> depth_level + 1, 1)
        distance = 2**depth_level
        entries.append((distance, slot_start, block_count))
        entries.append((-distance, slot_start + block_count, block_count))
        slot_start = slot_start + 2 * block_count
    return entries


def sender_ids(key_blocks, frame_rank, frames, blocks_dev, shift_by, slot_start, block_count):
    reader = jnp.clip(frame_rank + shift_by, 0, frames - 1)
    reader_row = lax.dynamic_slice_in_dim(key_blocks, reader, 1, 0)[0]
    listed = reader_row[slot_start : slot_start + block_count]
    return jnp.clip(listed - frame_rank * blocks_dev, 0, blocks_dev - 1)


def pack_kernel(counts, ids_ref, k_ref, v_ref, *out_refs):
    at = 0
    for out_ref, count in zip(out_refs, counts):
        for j in range(count):
            start = pl.multiple_of(ids_ref[at] * BLOCK, BLOCK)
            at += 1
            rows = slice(j * BLOCK, (j + 1) * BLOCK)
            out_ref[0, 0, rows, :] = k_ref[pl.ds(start, BLOCK), :]
            out_ref[0, 1, rows, :] = v_ref[pl.ds(start, BLOCK), :]


def contract(a, b, dim_a, dim_b):
    return lax.dot_general(
        a, b, (((dim_a,), (dim_b,)), ((), ())), preferred_element_type=jnp.float32
    )


def fold_rows(x, op):
    total = x[0:8]
    for r in range(8, x.shape[0], 8):
        total = op(total, x[r : r + 8])
    return total


def main_kernel(entries, spans, frames, heads, *refs):
    n_win = len(spans)
    rk_ref, kt_ref, bias_ref, q_ref, k_ref, v_ref, do_ref = refs[:7]
    packed_refs = refs[7 : 7 + n_win]
    outs = refs[7 + n_win :]
    att_ref, dq_ref, own_ref = outs[:3]
    ret_refs = outs[3 : 3 + n_win]
    scratch = outs[3 + n_win :]
    kall, vall, s_ref, dp_ref, pd_ref, ds_ref, gk_ref, gv_ref = scratch[:8]
    win_refs = scratch[8 : 8 + n_win]
    back_refs = scratch[8 + n_win : 8 + 2 * n_win]
    fetch_send, fetch_recv, back_send, back_recv = scratch[8 + 2 * n_win :]
    tok = q_ref.shape[0]
    slots = kall.shape[0]
    score_scale = 1.0 / math.sqrt(HD)
    exp_scale = score_scale * math.log2(math.e)
    steps = slots // ROWS
    tiles = tok // 128
    head = pl.program_id(0)
    rank = lax.axis_index("frame")
    distances = [entry[0] for entry in entries]

    def present(other):
        return jnp.logical_and(other >= 0, other < frames)

    def fetch(w, h):
        return pltpu.make_async_remote_copy(
            src_ref=packed_refs[w].at[h], dst_ref=win_refs[w].at[h],
            send_sem=fetch_send.at[w, h], recv_sem=fetch_recv.at[w, h],
            device_id={"frame": lax.rem(rank + distances[w] + frames, frames)}, device_id_type=pl.DeviceIdType.MESH,
        )

    def give_back(w, h):
        return pltpu.make_async_remote_copy(
            src_ref=back_refs[w].at[h], dst_ref=ret_refs[w].at[h],
            send_sem=back_send.at[w, h], recv_sem=back_recv.at[w, h],
            device_id={"frame": lax.rem(rank - distances[w] + frames, frames)}, device_id_type=pl.DeviceIdType.MESH,
        )

    @pl.when(head == 0)
    def _():
        barrier = pltpu.get_barrier_semaphore()
        for d in distances:
            @pl.when(present(rank + d))
            def _(d=d):
                pl.semaphore_signal(
                    barrier, inc=1, device_id={"frame": rank + d},
                    device_id_type=pl.DeviceIdType.MESH,
                )
        peers = jnp.int32(0)
        for d in distances:
            peers = peers + present(rank + d).astype(jnp.int32)
        pl.semaphore_wait(barrier, peers)

        def send_head(h, _):
            for w, d in enumerate(distances):
                @pl.when(present(rank + d))
                def _(w=w):
                    fetch(w, h).start()
            return 0

        lax.fori_loop(0, heads, send_head, 0)

    kall[0:tok, :] = k_ref[...]
    vall[0:tok, :] = v_ref[...]
    for w, (lo, hi) in enumerate(spans):
        @pl.when(present(rank - distances[w]))
        def _(w=w, lo=lo, hi=hi):
            fetch(w, head).wait_recv()
            kall[lo:hi, :] = win_refs[w][head, 0]
            vall[lo:hi, :] = win_refs[w][head, 1]

        @pl.when(jnp.logical_not(present(rank - distances[w])))
        def _(lo=lo, hi=hi):
            kall[lo:hi, :] = jnp.zeros((hi - lo, HD), jnp.bfloat16)
            vall[lo:hi, :] = jnp.zeros((hi - lo, HD), jnp.bfloat16)

    def rows_of(j):
        return pl.ds(pl.multiple_of(j * ROWS, ROWS), ROWS)

    def pass_a(j, top):
        rows = rows_of(j)
        raw = contract(kall[rows, :], q_ref[...], 1, 1)
        bias = bias_ref[rows, :]
        new_top = []
        for t in range(tiles):
            lanes = slice(t * 128, (t + 1) * 128)
            s = raw[:, lanes] + bias
            s_ref[rows, lanes] = s
            new_top.append(jnp.maximum(top[t], fold_rows(s, jnp.maximum)))
        return tuple(new_top)

    top = lax.fori_loop(
        0, steps, pass_a, tuple(jnp.full((8, 128), -jnp.inf, jnp.float32) for _ in range(tiles))
    )
    top = [jnp.max(t, axis=0, keepdims=True) for t in top]
    head_term = head * 977
    row_keys = [rk_ref[:, t * 128 : (t + 1) * 128] for t in range(tiles)]

    def pass_b(j, sums):
        rows = rows_of(j)
        grads = contract(vall[rows, :], do_ref[...], 1, 1)
        token_term = kt_ref[rows, :] + head_term
        new_sums = []
        for t in range(tiles):
            lanes = slice(t * 128, (t + 1) * 128)
            e = jnp.exp2((s_ref[rows, lanes] - top[t]) * exp_scale)
            x = token_term ^ row_keys[t]
            x = x * -1640531535
            x = x ^ logical_right(x, 16)
            x = x * 739982445
            x = x ^ logical_right(x, 15)
            keep = (x & (1023 << 16)) >= (102 << 16)
            dp = grads[:, lanes]
            dp_ref[rows, lanes] = dp
            s_ref[rows, lanes] = jnp.where(keep, e, -e)
            kept = jnp.where(keep, e * dp, 0.0)
            new_sums.append(sums[2 * t] + fold_rows(e, jnp.add))
            new_sums.append(sums[2 * t + 1] + fold_rows(kept, jnp.add))
        return tuple(new_sums)

    sums = lax.fori_loop(
        0, steps, pass_b, tuple(jnp.zeros((8, 128), jnp.float32) for _ in range(2 * tiles))
    )
    sums = [jnp.sum(x, axis=0, keepdims=True) for x in sums]
    inv = [KEEP_SCALE / sums[2 * t] for t in range(tiles)]
    inv_scaled = [x * score_scale for x in inv]
    delta = [sums[2 * t + 1] * inv[t] * (inv_scaled[t] / KEEP_SCALE) for t in range(tiles)]

    def pass_c(j, _):
        rows = rows_of(j)
        for t in range(tiles):
            lanes = slice(t * 128, (t + 1) * 128)
            es = s_ref[rows, lanes]
            kept = jnp.maximum(es, 0.0)
            pd = kept * inv[t]
            ds = kept * inv_scaled[t] * dp_ref[rows, lanes] - jnp.abs(es) * delta[t]
            pd_ref[rows, lanes] = pd.astype(jnp.bfloat16)
            ds_ref[rows, lanes] = ds.astype(jnp.bfloat16)
        gk_ref[rows, :] = contract(ds_ref[rows, :], q_ref[...], 1, 0)
        gv_ref[rows, :] = contract(pd_ref[rows, :], do_ref[...], 1, 0)
        return 0

    lax.fori_loop(0, steps, pass_c, 0)
    own_ref[0] = gk_ref[0:tok, :]
    own_ref[1] = gv_ref[0:tok, :]
    for back_ref, (lo, hi) in zip(back_refs, spans):
        back_ref[head, 0] = gk_ref[lo:hi, :].astype(jnp.bfloat16)
        back_ref[head, 1] = gv_ref[lo:hi, :].astype(jnp.bfloat16)
    att_ref[...] = contract(pd_ref[...], vall[...], 0, 0).astype(jnp.bfloat16)
    dq_ref[...] = contract(ds_ref[...], kall[...], 0, 0).astype(jnp.bfloat16)
    for w, d in enumerate(distances):
        @pl.when(present(rank - d))
        def _(w=w):
            give_back(w, head).start()

    @pl.when(head == heads - 1)
    def _():
        def drain(h, _):
            for w, d in enumerate(distances):
                @pl.when(present(rank + d))
                def _(w=w):
                    fetch(w, h).wait_send()
                    give_back(w, h).wait_recv()

                @pl.when(present(rank - d))
                def _(w=w):
                    give_back(w, h).wait_send()
            return 0

        lax.fori_loop(0, heads, drain, 0)


def finish_kernel(counts, ids_ref, live_ref, own_ref, *refs):
    ret_refs = refs[: len(counts)]
    kg_ref, vg_ref, acc = refs[len(counts) :]
    acc[...] = own_ref[...]
    at = 0
    for w, (ret_ref, count) in enumerate(zip(ret_refs, counts)):
        @pl.when(live_ref[w] > 0)
        def _(ret_ref=ret_ref, count=count, at=at):
            for j in range(count):
                rows = pl.ds(pl.multiple_of(ids_ref[at + j] * BLOCK, BLOCK), BLOCK)
                part = ret_ref[0, :, j * BLOCK : (j + 1) * BLOCK, :]
                acc[:, rows, :] += part.astype(jnp.float32)
        at += count
    kg_ref[...] = acc[0].astype(jnp.bfloat16)
    vg_ref[...] = acc[1].astype(jnp.bfloat16)


def local(queries, keys, values, out_grad, key_blocks, seed_offsets, dropout_seed):
    tok, width = queries.shape
    blocks_dev = tok // BLOCK
    heads = width // HD
    frames = lax.axis_size("frame")
    frame_rank = lax.axis_index("frame")
    entries = plan_windows(blocks_dev)
    counts = [count for _, _, count in entries]
    spans = [(start * BLOCK, (start + count) * BLOCK) for _, start, count in entries]
    slots = key_blocks.shape[1] * BLOCK
    ids = jnp.concatenate(
        [sender_ids(key_blocks, frame_rank, frames, blocks_dev, *entry) for entry in entries]
    )
    listed = lax.dynamic_slice_in_dim(key_blocks, frame_rank, 1, 0)[0]
    alive = listed >= 0
    tokens = (jnp.where(alive, listed, 0)[:, None] * BLOCK + jnp.arange(BLOCK, dtype=jnp.int32)).reshape(-1)
    token_terms = jnp.broadcast_to((tokens * 40503)[:, None], (slots, 128))
    bias = jnp.where(jnp.repeat(alive, BLOCK), 0.0, -jnp.inf).astype(jnp.float32)
    bias = jnp.broadcast_to(bias[:, None], (slots, 128))
    query_tokens = frame_rank * tok + jnp.arange(tok, dtype=jnp.int32)
    row_keys = mixing(dropout_seed[0] + jnp.repeat(seed_offsets, BLOCK) + query_tokens * 7919)[None, :]

    bf16, f32 = jnp.bfloat16, jnp.float32
    smem = pl.BlockSpec(memory_space=pltpu.SMEM)
    anyspec = pl.BlockSpec(memory_space=pl.ANY)
    win_shapes = [jax.ShapeDtypeStruct((heads, 2, n * BLOCK, HD), bf16) for n in counts]
    win_specs = [pl.BlockSpec((1, 2, n * BLOCK, HD), lambda h: (h, 0, 0, 0)) for n in counts]
    full = jax.ShapeDtypeStruct((tok, width), bf16)
    column = pl.BlockSpec((tok, HD), lambda h: (0, h))
    own_spec = pl.BlockSpec((2, tok, HD), lambda h: (0, 0, h))
    table = pl.BlockSpec((slots, 128), lambda h: (0, 0))
    n_win = len(entries)
    reach = frame_rank + jnp.array([entry[0] for entry in entries], jnp.int32)
    live = jnp.logical_and(reach >= 0, reach < frames).astype(jnp.int32)

    packed = pl.pallas_call(
        functools.partial(pack_kernel, counts),
        grid=(heads,),
        in_specs=[smem, column, column],
        out_specs=win_specs,
        out_shape=win_shapes,
        name="pack",
    )(ids, keys, values)
    result = pl.pallas_call(
        functools.partial(main_kernel, entries, spans, frames, heads),
        grid=(heads,),
        in_specs=[
            pl.BlockSpec((1, tok), lambda h: (0, 0)), table, table,
            column, column, column, column, *([anyspec] * n_win),
        ],
        out_specs=[column, column, own_spec, *([anyspec] * n_win)],
        out_shape=[full, full, jax.ShapeDtypeStruct((2, tok, width), f32), *win_shapes],
        scratch_shapes=[
            pltpu.VMEM((slots, HD), bf16),
            pltpu.VMEM((slots, HD), bf16),
            pltpu.VMEM((slots, tok), f32),
            pltpu.VMEM((slots, tok), f32),
            pltpu.VMEM((slots, tok), bf16),
            pltpu.VMEM((slots, tok), bf16),
            pltpu.VMEM((slots, HD), f32),
            pltpu.VMEM((slots, HD), f32),
            *[pltpu.VMEM(shape.shape, bf16) for shape in win_shapes],
            *[pltpu.VMEM(shape.shape, bf16) for shape in win_shapes],
            *([pltpu.SemaphoreType.DMA((n_win, heads))] * 4),
        ],
        compiler_params=pltpu.CompilerParams(
            dimension_semantics=("arbitrary",), collective_id=0, has_side_effects=True
        ),
        name="attend",
    )(row_keys, token_terms, bias, queries, keys, values, out_grad, *packed)
    grads = pl.pallas_call(
        functools.partial(finish_kernel, counts),
        grid=(heads,),
        in_specs=[smem, smem, own_spec, *win_specs],
        out_specs=[column, column],
        out_shape=[full, full],
        scratch_shapes=[pltpu.VMEM((2, tok, HD), f32)],
        name="finish",
    )(ids, live, result[2], *result[3:])
    return (result[0], result[1], grads[0], grads[1])


def solution(mesh):
    rows = P(("rep", "frame"), None)
    return jax.shard_map(
        local,
        mesh=mesh,
        in_specs=(rows, rows, rows, rows, P("rep", None), P(("rep", "frame")), P("rep")),
        out_specs=(rows, rows, rows, rows),
        check_vma=False,
    )
```
